32 devices in a mesh: fsdp: 16 (over z, y, x), dp: 2 (over core).
Axes of the slice: x: 2, y: 2, z: 4, core: 2. Of those that a mesh axis runs over, the one named last changes fastest.
Arguments:
- grads: bfloat16 [2, 1024, 28672], P('dp', 'fsdp')
- block_slot: int32 [28], replicated, may hold values from 0 to 31, as said below
- left_stats: float32 [32, 1024, 1024], P('fsdp', 'dp')
- right_stats: float32 [32, 1024, 1024], P('fsdp', 'dp')
- left_root: bfloat16 [32, 1024, 1024], P('fsdp', 'dp')
- right_root: bfloat16 [32, 1024, 1024], P('fsdp', 'dp')
Outputs:
- left_new: float32 [32, 1024, 1024], P('fsdp', 'dp')
- right_new: float32 [32, 1024, 1024], P('fsdp', 'dp')
- update: bfloat16 [1024, 28672], P('fsdp')
The draws below stay inside these ranges and needn't reach their ends.
Inputs may be any that keep to these rules, and one draw needn't show every extreme that they name: The entries of block_slot are distinct. Block b's statistics and roots sit in slot block_slot[b], which belongs to the fsdp device of index block_slot[b] // 2; slots that no block names are empty and their statistics pass through unchanged.
All inputs are finite; a program needn't handle non-finite values.
Results may differ from the reference program's by a relative error of at most 0.015.
Values may be sent and summed in bfloat16 or wider, within the bound.
A program may use at most 128 MiB of HBM per device.

```python
import math
import jax
import jax.numpy as jnp
from jax import lax

BLOCK = 1024
COLS = 28672
REPLICAS = 2
SLOTS = 2
SLOT_TOTAL = 32
N_FSDP = 16


def scaled_log(key, shape, low, high):
    return jnp.exp(jax.random.uniform(key, shape, jnp.float32, math.log(low), math.log(high)))


def draw_grads(key, part):
    keys = jax.random.split(jax.random.fold_in(key, 11), 3)
    row_scale = scaled_log(keys[0], (BLOCK,), 1.0, 4.0)
    col_scale = scaled_log(keys[1], (COLS,), 1.0, 4.0)
    noise = jax.random.normal(keys[2], (REPLICAS, BLOCK, COLS), jnp.float32)
    values = 0.004 * noise * row_scale[None, :, None] * col_scale[None, None, :]
    return values.astype(jnp.bfloat16)


def draw_block_slot(key, part):
    order = jax.random.permutation(jax.random.fold_in(key, 23), SLOT_TOTAL)
    return order[:COLS // BLOCK].astype(jnp.int32)


def definite(key, low, high, spread):
    keys = jax.random.split(key, 2)
    diagonal = scaled_log(keys[0], (SLOT_TOTAL, BLOCK), low, high)
    noise = jax.random.normal(keys[1], (SLOT_TOTAL, BLOCK, BLOCK), jnp.float32)
    symmetric = (noise + jnp.swapaxes(noise, 1, 2)) * (spread / math.sqrt(2.0 * BLOCK))
    return symmetric + diagonal[:, :, None] * jnp.eye(BLOCK, dtype=jnp.float32)[None]


def draw_left_stats(key, part):
    return definite(jax.random.fold_in(key, 31), 1.0, 4.0, 0.8)


def draw_right_stats(key, part):
    return definite(jax.random.fold_in(key, 37), 1.0, 4.0, 0.8)


def draw_left_root(key, part):
    return definite(jax.random.fold_in(key, 41), 0.5, 1.5, 0.3).astype(jnp.bfloat16)


def draw_right_root(key, part):
    return definite(jax.random.fold_in(key, 43), 0.5, 1.5, 0.3).astype(jnp.bfloat16)


def setup_inputs(seed: int = 0) -> dict:
    key_of = jax.random.split(jax.random.key(seed), 7)
    return {
        "grads": draw_grads(jax.random.fold_in(key_of[6], 71), 0),
        "block_slot": draw_block_slot(jax.random.fold_in(key_of[6], 71), 0),
        "left_stats": draw_left_stats(jax.random.fold_in(key_of[6], 71), 0),
        "right_stats": draw_right_stats(jax.random.fold_in(key_of[6], 71), 0),
        "left_root": draw_left_root(jax.random.fold_in(key_of[6], 71), 0),
        "right_root": draw_right_root(jax.random.fold_in(key_of[6], 71), 0),
    }


epsilon = 1e-06

def reference(grads, block_slot, left_stats, right_stats, left_root, right_root):
    block_count = COLS // BLOCK
    total_slots = SLOTS * N_FSDP
    summed = lax.optimization_barrier(jnp.sum(grads.astype(jnp.float32), axis=0)).astype(jnp.bfloat16)
    gradient = summed.reshape(BLOCK, block_count, BLOCK).transpose(1, 0, 2)
    numbers = jnp.arange(block_count, dtype=jnp.int32)

    def statistics(slot_id):
        matches = block_slot == slot_id
        filled = jnp.any(matches)
        position = jnp.sum(jnp.where(matches, numbers, 0)).astype(jnp.int32)
        chosen = jnp.where(filled, gradient[position], jnp.zeros((), jnp.bfloat16))
        left_sum = left_stats[slot_id] + jnp.dot(chosen, chosen.T, preferred_element_type=jnp.float32)
        right_sum = right_stats[slot_id] + jnp.dot(chosen.T, chosen, preferred_element_type=jnp.float32)
        return (left_sum, right_sum)
    left_new, right_new = lax.map(statistics, jnp.arange(total_slots, dtype=jnp.int32))

    def precondition(operands):
        one_block, slot_id = operands
        left_applied = jnp.dot(left_root[slot_id], one_block, preferred_element_type=jnp.float32).astype(jnp.bfloat16)
        both_applied = jnp.dot(left_applied, right_root[slot_id], preferred_element_type=jnp.float32)
        return (both_applied * lax.rsqrt(jnp.mean(both_applied * both_applied) + epsilon)).astype(jnp.bfloat16)
    updates = lax.map(precondition, (gradient, block_slot))
    update = updates.transpose(1, 0, 2).reshape(BLOCK, COLS)
    return (left_new, right_new, update)
```

```python
import functools
import jax
import jax.numpy as jnp
from jax import lax
from jax.experimental import pallas as pl
from jax.experimental.pallas import tpu as pltpu
from jax.sharding import PartitionSpec as P

epsilon = 1e-06
VMEM_BYTES = 60 * 1024 * 1024


def exchange_kernel(
    sizes,
    source_ref,
    grads_hbm,
    left_hbm,
    right_hbm,
    gradient_out,
    returned_out,
    factor_out,
    grads,
    outgoing,
    incoming,
    summed,
    gradient,
    left,
    right,
    total,
    applied,
    factor,
    load_sem,
    local_sem,
    root_send,
    root_recv,
    swap_send,
    swap_recv,
    there_send,
    there_recv,
    back_send,
    back_recv,
    relay_send,
    relay_recv,
    factor_send,
    factor_recv,
    whole_send,
    whole_recv,
):
    owners, cores, rows, size, group = sizes
    groups = owners // group
    depth = group * rows
    half = size // cores
    me = lax.axis_index("fsdp")
    core = lax.axis_index("dp")
    other = 1 - core
    my_group = me // group
    my_place = me % group
    far_first = [groups // 2] + [d for d in range(groups - 1, 0, -1) if d != groups // 2] + [0]
    near_first = [0] + far_first[:-1]

    def target(shift, step):
        return ((my_group + shift) % groups) * group + (my_place + step) % group

    def origin(shift, step):
        return ((my_group + groups - shift) % groups) * group + (my_place + group - step) % group

    def block_rows(device):
        return pl.ds(pl.multiple_of(device * rows, rows), rows)

    def chosen(slot):
        return grads[source_ref[slot]]

    def remote(src, dst, send, recv, owner, to_core):
        return pltpu.make_async_remote_copy(
            src_ref=src,
            dst_ref=dst,
            send_sem=send,
            recv_sem=recv,
            device_id={"fsdp": owner, "dp": to_core},
            device_id_type=pl.DeviceIdType.MESH,
        )

    def load(block, carry):
        columns = pl.ds(pl.multiple_of(block * size, size), size)
        pltpu.make_async_copy(grads_hbm.at[0, :, columns], grads.at[block], load_sem).start()
        return carry

    lax.fori_loop(0, grads.shape[0], load, 0)
    barrier = pltpu.get_barrier_semaphore()
    pl.semaphore_signal(
        barrier,
        inc=1,
        device_id={"fsdp": me, "dp": other},
        device_id_type=pl.DeviceIdType.MESH,
    )

    def greet(step, carry):
        pl.semaphore_signal(
            barrier,
            inc=1,
            device_id={"fsdp": (me + step) % owners, "dp": core},
            device_id_type=pl.DeviceIdType.MESH,
        )
        return carry

    lax.fori_loop(1, owners, greet, 0)
    own_half = pl.ds(pl.multiple_of(core * half, half), half)
    other_half = pl.ds(pl.multiple_of(other * half, half), half)
    keep_left = pltpu.make_async_copy(left_hbm.at[core], left.at[own_half], local_sem.at[0])
    keep_right = pltpu.make_async_copy(right_hbm.at[core], right.at[own_half], local_sem.at[1])
    keep_left.start()
    keep_right.start()
    pltpu.make_async_copy(grads, grads, load_sem).wait()

    def pick(device, carry):
        outgoing[device] = chosen(device * cores + other)
        return carry

    lax.fori_loop(0, owners, pick, 0)
    pl.semaphore_wait(barrier, owners)

    def swap(device, index):
        return remote(
            outgoing.at[device],
            incoming.at[device],
            swap_send.at[index],
            swap_recv.at[index],
            me,
            other,
        )

    for order, shift in enumerate(far_first):

        def start_swap(step, carry):
            swap(target(shift, step), order * group + step).start()
            return carry

        lax.fori_loop(0, group, start_swap, 0)

    give_left = remote(
        left_hbm.at[other], left.at[own_half], root_send.at[0], root_recv.at[0], me, other
    )
    give_right = remote(
        right_hbm.at[other], right.at[own_half], root_send.at[1], root_recv.at[1], me, other
    )
    give_left.start()
    give_right.start()

    def there(device, index):
        return remote(
            summed.at[device],
            gradient.at[block_rows(me)],
            there_send.at[index],
            there_recv.at[index],
            device,
            core,
        )

    def summed_block(device, index):
        mine = chosen(device * cores + core)
        swap(device, index).wait_recv()
        return (mine.astype(jnp.float32) + incoming[device].astype(jnp.float32)).astype(
            jnp.bfloat16
        )

    for order, shift in enumerate(far_first):

        def start_there(step, carry):
            device = target(shift, step)
            index = order * group + step
            summed[device] = summed_block(device, index)
            there(device, index).start()
            return carry

        lax.fori_loop(0 if shift else 1, group, start_there, 0)
    gradient[block_rows(me)] = summed_block(me, (groups - 1) * group)

    keep_left.wait()
    keep_right.wait()
    give_left.wait_recv()
    give_right.wait_recv()

    def wait_there(shift):
        order = far_first.index(shift)

        def body(step, carry):
            there(me, order * group + step).wait_recv()
            return carry

        lax.fori_loop(0 if shift else 1, group, body, 0)

    def group_rows(index):
        return pl.ds(pl.multiple_of(index * depth, depth), depth)

    for order, shift in enumerate(near_first[:-1]):
        wait_there(shift)
        deep = group_rows((my_group + groups - shift) % groups)

        def accumulate(index, carry):
            part = jnp.dot(
                left[group_rows(index), deep],
                gradient[deep],
                preferred_element_type=jnp.float32,
            )
            if order:
                part = part + total[group_rows(index)]
            total[group_rows(index)] = part
            return carry

        lax.fori_loop(0, groups, accumulate, 0)

    wait_there(near_first[-1])
    deep = group_rows((my_group + groups - near_first[-1]) % groups)

    def back(device, index):
        return remote(
            applied.at[block_rows(device)],
            returned_out.at[core, me],
            back_send.at[index],
            back_recv.at[index],
            device,
            core,
        )

    squares = jnp.zeros((1, size), jnp.float32)
    for order, shift in enumerate(far_first):
        out_rows = group_rows((my_group + shift) % groups)
        left_applied = jnp.dot(
            left[out_rows, deep], gradient[deep], preferred_element_type=jnp.float32
        )
        left_applied = (left_applied + total[out_rows]).astype(jnp.bfloat16)
        both = jnp.dot(left_applied, right[...], preferred_element_type=jnp.float32)
        squares = squares + jnp.sum(both * both, axis=0, keepdims=True)
        applied[out_rows] = both.astype(jnp.bfloat16)

        def start_back(step, carry):
            back(target(shift, step), order * group + step).start()
            return carry

        lax.fori_loop(0 if shift else 1, group, start_back, 0)

    scale = lax.rsqrt(jnp.sum(squares, axis=1, keepdims=True) / (size * size) + epsilon)
    factor[...] = jnp.broadcast_to(scale, factor.shape)

    def give_factor(device, index):
        return remote(
            factor,
            factor_out.at[core, me],
            factor_send.at[index],
            factor_recv.at[index],
            device,
            core,
        )

    def start_factor(step, carry):
        give_factor((me + step) % owners, step).start()
        return carry

    lax.fori_loop(1, owners, start_factor, 0)
    keep_factor = pltpu.make_async_copy(factor, factor_out.at[core, me], local_sem.at[0])
    keep_factor.start()
    keep_gradient = pltpu.make_async_copy(gradient, gradient_out.at[core], local_sem.at[1])
    keep_gradient.start()
    keep_back = pltpu.make_async_copy(
        applied.at[block_rows(me)], returned_out.at[core, me], local_sem.at[2]
    )
    keep_back.start()
    own_relay = remote(
        applied.at[block_rows(me)],
        returned_out.at[core, me],
        relay_send.at[(groups - 1) * group],
        relay_recv.at[(groups - 1) * group],
        me,
        other,
    )
    own_relay.start()
    give_gradient = remote(
        gradient, gradient_out.at[core], whole_send.at[0], whole_recv.at[0], me, other
    )
    give_gradient.start()

    def relay(device, index):
        return remote(
            returned_out.at[core, device],
            returned_out.at[core, device],
            relay_send.at[index],
            relay_recv.at[index],
            me,
            other,
        )

    for shift in near_first:
        order = far_first.index(shift)

        def start_relay(step, carry):
            index = order * group + step
            back(me, index).wait_recv()
            relay(origin(shift, step), index).start()
            return carry

        lax.fori_loop(0 if shift else 1, group, start_relay, 0)

    def wait_factor(step, carry):
        give_factor(me, step).wait_recv()
        return carry

    lax.fori_loop(1, owners, wait_factor, 0)
    keep_factor.wait()
    whole_factor = remote(
        factor_out.at[core], factor_out.at[core], whole_send.at[1], whole_recv.at[1], me, other
    )
    whole_factor.start()

    def drain(index, carry):
        swap(me, index).wait_send()
        relay(me, index).wait()
        return carry

    lax.fori_loop(0, owners, drain, 0)

    def drain_far(index, carry):
        there(me, index).wait_send()
        back(me, index).wait_send()
        return carry

    lax.fori_loop(0, (groups - 1) * group, drain_far, 0)
    lax.fori_loop((groups - 1) * group + 1, owners, drain_far, 0)

    def drain_factor(step, carry):
        give_factor(me, step).wait_send()
        return carry

    lax.fori_loop(1, owners, drain_factor, 0)
    give_left.wait_send()
    give_right.wait_send()
    keep_gradient.wait()
    keep_back.wait()
    give_gradient.wait()
    whole_factor.wait()


def exchange(source, grads, left_root, right_root):
    slots, half, size = left_root.shape
    rows = grads.shape[1]
    owners = lax.axis_size("fsdp")
    cores = lax.axis_size("dp")
    group = max(1, min(owners, 256 // rows))
    dma = pltpu.SemaphoreType.DMA
    bf16 = jnp.bfloat16
    anywhere = pl.BlockSpec(memory_space=pl.ANY)
    return pl.pallas_call(
        functools.partial(exchange_kernel, (owners, cores, rows, size, group)),
        out_shape=(
            jax.ShapeDtypeStruct((cores, size, size), bf16),
            jax.ShapeDtypeStruct((cores, owners, rows, size), bf16),
            jax.ShapeDtypeStruct((cores, owners, 8, 128), jnp.float32),
        ),
        in_specs=[pl.BlockSpec(memory_space=pltpu.SMEM)] + [anywhere] * 3,
        out_specs=(anywhere,) * 3,
        scratch_shapes=[
            pltpu.VMEM((grads.shape[2] // size, rows, size), bf16),
            pltpu.VMEM((owners, rows, size), bf16),
            pltpu.VMEM((owners, rows, size), bf16),
            pltpu.VMEM((owners, rows, size), bf16),
            pltpu.VMEM((size, size), bf16),
            pltpu.VMEM((size, size), bf16),
            pltpu.VMEM((size, size), bf16),
            pltpu.VMEM((size, size), jnp.float32),
            pltpu.VMEM((size, size), bf16),
            pltpu.VMEM((8, 128), jnp.float32),
            dma,
            dma((3,)),
            dma((2,)),
            dma((2,)),
        ]
        + [dma((owners,))] * 10
        + [dma((2,)), dma((2,))],
        compiler_params=pltpu.CompilerParams(
            collective_id=0, has_side_effects=True, vmem_limit_bytes=VMEM_BYTES
        ),
    )(source, grads, left_root, right_root)


def statistics_kernel(tile, place_ref, filled_ref, gradient, left_in, right_in, left_out, right_out):
    size = gradient.shape[1]
    start = place_ref[0] * left_in.shape[1] * pl.num_programs(1) + pl.program_id(1) * tile
    part = pl.ds(pl.multiple_of(start, tile), tile)
    filled = filled_ref[place_ref[1] + pl.program_id(0)] > 0
    left_gram = lax.dot_general(
        gradient[0, part, :],
        gradient[0],
        (((1,), (1,)), ((), ())),
        preferred_element_type=jnp.float32,
    )
    left_out[0] = left_in[0] + jnp.where(filled, left_gram, 0.0)
    right_gram = lax.dot_general(
        gradient[0, :, part],
        gradient[0],
        (((0,), (0,)), ((), ())),
        preferred_element_type=jnp.float32,
    )
    right_out[0] = right_in[0] + jnp.where(filled, right_gram, 0.0)


def statistics(filled, gradient, left_stats, right_stats):
    slots, half, size = left_stats.shape
    tile = min(half, 256)
    place = jnp.stack([lax.axis_index("dp"), lax.axis_index("fsdp") * slots]).astype(jnp.int32)
    whole = pl.BlockSpec((1, size, size), lambda s, r, p, f: (s, 0, 0))
    band = pl.BlockSpec((1, tile, size), lambda s, r, p, f: (s, r, 0))
    out = jax.ShapeDtypeStruct(left_stats.shape, jnp.float32)
    return pl.pallas_call(
        functools.partial(statistics_kernel, tile),
        out_shape=(out, out),
        grid_spec=pltpu.PrefetchScalarGridSpec(
            num_scalar_prefetch=2,
            grid=(slots, half // tile),
            in_specs=[whole, band, band],
            out_specs=(band, band),
        ),
        compiler_params=pltpu.CompilerParams(vmem_limit_bytes=VMEM_BYTES),
    )(place, filled, gradient, left_stats, right_stats)


def assemble_kernel(count, slot_ref, returned, factor, update):
    cores, size = returned.shape[0], returned.shape[3]
    for index in range(count):
        slot = slot_ref[pl.program_id(0) * count + index]
        owner, core = slot // cores, slot % cores
        scale = factor[core, owner][:1, :1]
        piece = returned[core, owner].astype(jnp.float32) * scale
        update[:, index * size : (index + 1) * size] = piece.astype(update.dtype)


def assemble(block_slot, returned, factor):
    cores, owners, rows, size = returned.shape
    blocks = block_slot.shape[0]
    steps = next(n for n in (4, 2, 1) if blocks % n == 0)
    count = blocks // steps
    return pl.pallas_call(
        functools.partial(assemble_kernel, count),
        out_shape=jax.ShapeDtypeStruct((rows, blocks * size), returned.dtype),
        grid_spec=pltpu.PrefetchScalarGridSpec(
            num_scalar_prefetch=1,
            grid=(steps,),
            in_specs=[
                pl.BlockSpec(returned.shape, lambda i, s: (0, 0, 0, 0)),
                pl.BlockSpec(factor.shape, lambda i, s: (0, 0, 0, 0)),
            ],
            out_specs=pl.BlockSpec((rows, count * size), lambda i, s: (0, i)),
        ),
        compiler_params=pltpu.CompilerParams(vmem_limit_bytes=VMEM_BYTES),
    )(block_slot, returned, factor)


def slot_per_core(grads, block_slot, left_stats, right_stats, left_root, right_root):
    block_count = block_slot.shape[0]
    total_slots = left_stats.shape[0] * lax.axis_size("fsdp")
    matches = block_slot[None, :] == jnp.arange(total_slots, dtype=jnp.int32)[:, None]
    numbers = jnp.arange(block_count, dtype=jnp.int32)
    source = jnp.sum(jnp.where(matches, numbers[None, :], 0), axis=1)
    filled = jnp.sum(matches.astype(jnp.int32), axis=1)
    gradient, returned, factor = exchange(source, grads, left_root, right_root)
    left_new, right_new = statistics(filled, gradient, left_stats, right_stats)
    return (left_new, right_new, assemble(block_slot, returned, factor))


def per_device(grads, block_slot, left_stats, right_stats, left_root, right_root):
    local_rows = grads[0]
    row_dev, col_count = local_rows.shape
    block_size = left_stats.shape[2]
    block_count = col_count // block_size
    slot_count = left_stats.shape[0]
    shared_rows = left_stats.shape[1]
    total_slots = slot_count * lax.axis_size("fsdp")
    slot_ids = jnp.arange(total_slots, dtype=jnp.int32)
    matches = block_slot[None, :] == slot_ids[:, None]
    filled = jnp.any(matches, axis=1)
    source = jnp.sum(
        jnp.where(matches, jnp.arange(block_count, dtype=jnp.int32)[None, :], 0), axis=1
    )
    row_start = lax.axis_index("dp") * shared_rows
    band = local_rows.astype(jnp.float32).reshape(row_dev, block_count, block_size)
    shares = lax.psum_scatter(band.astype(jnp.bfloat16), "dp", scatter_dimension=2, tiled=True)
    outgoing = jnp.where(
        filled[None, :, None], jnp.take(shares, source, axis=1), jnp.zeros((), jnp.bfloat16)
    )
    incoming = lax.all_to_all(outgoing, "fsdp", split_axis=1, concat_axis=0, tiled=True)
    gradient = lax.all_gather(incoming, "dp", axis=2, tiled=True)
    own_rows = lax.dynamic_slice_in_dim(gradient, row_start, shared_rows, 0)
    whole_right = lax.all_gather(right_root, "dp", axis=1, tiled=True)
    left_new = left_stats + jnp.einsum(
        "rjc,kjc->jrk", own_rows, gradient, preferred_element_type=jnp.float32
    )
    columns = lax.dynamic_slice_in_dim(gradient, row_start, shared_rows, 2)
    right_new = right_stats + jnp.einsum(
        "rjc,rjk->jck", columns, gradient, preferred_element_type=jnp.float32
    )
    left_applied = jnp.einsum(
        "jrk,kjc->rjc", left_root, gradient, preferred_element_type=jnp.float32
    ).astype(jnp.bfloat16)
    both_applied = jnp.einsum(
        "rjc,jck->rjk", left_applied, whole_right, preferred_element_type=jnp.float32
    )
    squares = lax.psum(jnp.sum(both_applied * both_applied, axis=(0, 2)), "dp")
    factor = lax.rsqrt(squares / (block_size * block_size) + epsilon)
    scaled = (both_applied * factor[None, :, None]).astype(jnp.bfloat16)
    full_rows = lax.all_gather(scaled, "dp", axis=0, tiled=True)
    returned = lax.all_to_all(full_rows, "fsdp", split_axis=0, concat_axis=1, tiled=True)
    update = jnp.take(returned, block_slot, axis=1).reshape(row_dev, col_count)
    return (left_new, right_new, update)


def per_shard(*args):
    grads, _, left_stats = args[:3]
    slots, rows = left_stats.shape[0], grads.shape[1]
    paired = slots == 2 and lax.axis_size("dp") == 2
    even = rows % 16 == 0 and 256 % rows == 0 and lax.axis_size("fsdp") % (256 // rows) == 0
    if paired and even:
        return slot_per_core(*args)
    return per_device(*args)


def solution(mesh):
    in_specs = (
        P("dp", "fsdp", None),
        P(),
        P("fsdp", "dp", None),
        P("fsdp", "dp", None),
        P("fsdp", "dp", None),
        P("fsdp", "dp", None),
    )
    out_specs = (P("fsdp", "dp", None), P("fsdp", "dp", None), P("fsdp", None))
    return jax.shard_map(
        per_shard, mesh=mesh, in_specs=in_specs, out_specs=out_specs, check_vma=False
    )
```

```python
import functools
import jax
import jax.numpy as jnp
from jax import lax
from jax.experimental import pallas as pl
from jax.experimental.pallas import tpu as pltpu
from jax.sharding import PartitionSpec as P

epsilon = 1e-06
VMEM_BYTES = 44 * 1024 * 1024
FINISH_BYTES = 28 * 1024 * 1024


def exchange_kernel(
    sizes,
    source_ref,
    filled_ref,
    grads_hbm,
    left_hbm,
    right_hbm,
    left_stats,
    right_stats,
    left_out,
    right_out,
    returned_out,
    factor_out,
    grads,
    outgoing,
    incoming,
    summed,
    gradients,
    left,
    right,
    total,
    applied,
    factor,
    load_sem,
    stats_sem,
    local_sem,
    root_send,
    root_recv,
    swap_send,
    swap_recv,
    there_send,
    there_recv,
    back_send,
    back_recv,
    relay_send,
    relay_recv,
    factor_send,
    factor_recv,
    whole_send,
    whole_recv,
):
    owners, cores, rows, size, group = sizes
    groups = owners // group
    depth = group * rows
    half = size // cores
    me = lax.axis_index("fsdp")
    core = lax.axis_index("dp")
    other = 1 - core
    gradient = gradients.at[core]
    my_group = me // group
    my_place = me % group
    far_first = [groups // 2] + [d for d in range(groups - 1, 0, -1) if d != groups // 2] + [0]
    near_first = [0] + far_first[:-1]

    def target(shift, step):
        return ((my_group + shift) % groups) * group + (my_place + step) % group

    def origin(shift, step):
        return ((my_group + groups - shift) % groups) * group + (my_place + group - step) % group

    def block_rows(device):
        return pl.ds(pl.multiple_of(device * rows, rows), rows)

    def chosen(slot):
        return grads[source_ref[slot]]

    def remote(src, dst, send, recv, owner, to_core):
        return pltpu.make_async_remote_copy(
            src_ref=src,
            dst_ref=dst,
            send_sem=send,
            recv_sem=recv,
            device_id={"fsdp": owner, "dp": to_core},
            device_id_type=pl.DeviceIdType.MESH,
        )

    def load(block, carry):
        columns = pl.ds(pl.multiple_of(block * size, size), size)
        pltpu.make_async_copy(grads_hbm.at[0, :, columns], grads.at[block], load_sem).start()
        return carry

    lax.fori_loop(0, grads.shape[0], load, 0)
    barrier = pltpu.get_barrier_semaphore()
    pl.semaphore_signal(
        barrier,
        inc=1,
        device_id={"fsdp": me, "dp": other},
        device_id_type=pl.DeviceIdType.MESH,
    )

    def greet(step, carry):
        pl.semaphore_signal(
            barrier,
            inc=1,
            device_id={"fsdp": (me + step) % owners, "dp": core},
            device_id_type=pl.DeviceIdType.MESH,
        )
        return carry

    lax.fori_loop(1, owners, greet, 0)
    own_half = pl.ds(pl.multiple_of(core * half, half), half)
    other_half = pl.ds(pl.multiple_of(other * half, half), half)
    keep_left = pltpu.make_async_copy(left_hbm.at[core], left.at[own_half], local_sem.at[0])
    keep_right = pltpu.make_async_copy(right_hbm.at[core], right.at[own_half], local_sem.at[1])
    keep_left.start()
    keep_right.start()
    read_left = pltpu.make_async_copy(left_stats, left_out, stats_sem.at[0])
    read_right = pltpu.make_async_copy(right_stats, right_out, stats_sem.at[1])
    read_left.start()
    read_right.start()
    pltpu.make_async_copy(grads, grads, load_sem).wait()

    def pick(device, carry):
        outgoing[device] = chosen(device * cores + other)
        return carry

    lax.fori_loop(0, owners, pick, 0)
    pl.semaphore_wait(barrier, owners)

    def swap(device, index):
        return remote(
            outgoing.at[device],
            incoming.at[device],
            swap_send.at[index],
            swap_recv.at[index],
            me,
            other,
        )

    for order, shift in enumerate(far_first):

        def start_swap(step, carry):
            swap(target(shift, step), order * group + step).start()
            return carry

        lax.fori_loop(0, group, start_swap, 0)

    give_left = remote(
        left_hbm.at[other], left.at[own_half], root_send.at[0], root_recv.at[0], me, other
    )
    give_right = remote(
        right_hbm.at[other], right.at[own_half], root_send.at[1], root_recv.at[1], me, other
    )
    give_left.start()
    give_right.start()

    def there(device, index):
        return remote(
            summed.at[device],
            gradient.at[block_rows(me)],
            there_send.at[index],
            there_recv.at[index],
            device,
            core,
        )

    def summed_block(device, index):
        mine = chosen(device * cores + core)
        swap(device, index).wait_recv()
        return (mine.astype(jnp.float32) + incoming[device].astype(jnp.float32)).astype(
            jnp.bfloat16
        )

    for order, shift in enumerate(far_first):

        def start_there(step, carry):
            device = target(shift, step)
            index = order * group + step
            summed[device] = summed_block(device, index)
            there(device, index).start()
            return carry

        lax.fori_loop(0 if shift else 1, group, start_there, 0)
    gradient[block_rows(me)] = summed_block(me, (groups - 1) * group)

    keep_left.wait()
    keep_right.wait()
    give_left.wait_recv()
    give_right.wait_recv()

    def wait_there(shift):
        order = far_first.index(shift)

        def body(step, carry):
            there(me, order * group + step).wait_recv()
            return carry

        lax.fori_loop(0 if shift else 1, group, body, 0)

    def group_rows(index):
        return pl.ds(pl.multiple_of(index * depth, depth), depth)

    for order, shift in enumerate(near_first[:-1]):
        wait_there(shift)
        deep = group_rows((my_group + groups - shift) % groups)

        def accumulate(index, carry):
            part = jnp.dot(
                left[group_rows(index), deep],
                gradient[deep],
                preferred_element_type=jnp.float32,
            )
            if order:
                part = part + total[group_rows(index)]
            total[group_rows(index)] = part
            return carry

        lax.fori_loop(0, groups, accumulate, 0)

    wait_there(near_first[-1])
    deep = group_rows((my_group + groups - near_first[-1]) % groups)

    def back(device, index):
        return remote(
            applied.at[block_rows(device)],
            returned_out.at[core, me],
            back_send.at[index],
            back_recv.at[index],
            device,
            core,
        )

    give_gradient = remote(gradient, gradient, whole_send.at[0], whole_recv.at[0], me, other)
    give_gradient.start()
    squares = jnp.zeros((1, size), jnp.float32)
    for order, shift in enumerate(far_first):
        out_rows = group_rows((my_group + shift) % groups)
        left_applied = jnp.dot(
            left[out_rows, deep], gradient[deep], preferred_element_type=jnp.float32
        )
        left_applied = (left_applied + total[out_rows]).astype(jnp.bfloat16)
        both = jnp.dot(left_applied, right[...], preferred_element_type=jnp.float32)
        squares = squares + jnp.sum(both * both, axis=0, keepdims=True)
        applied[out_rows] = both.astype(jnp.bfloat16)

        def start_back(step, carry):
            back(target(shift, step), order * group + step).start()
            return carry

        lax.fori_loop(0 if shift else 1, group, start_back, 0)

    scale = lax.rsqrt(jnp.sum(squares, axis=1, keepdims=True) / (size * size) + epsilon)
    factor[...] = jnp.broadcast_to(scale, factor.shape)

    def give_factor(device, index):
        return remote(
            factor,
            factor_out.at[core, me],
            factor_send.at[index],
            factor_recv.at[index],
            device,
            core,
        )

    def start_factor(step, carry):
        give_factor((me + step) % owners, step).start()
        return carry

    lax.fori_loop(1, owners, start_factor, 0)
    keep_factor = pltpu.make_async_copy(factor, factor_out.at[core, me], local_sem.at[0])
    keep_factor.start()
    keep_back = pltpu.make_async_copy(
        applied.at[block_rows(me)], returned_out.at[core, me], local_sem.at[2]
    )
    keep_back.start()
    own_relay = remote(
        applied.at[block_rows(me)],
        returned_out.at[core, me],
        relay_send.at[(groups - 1) * group],
        relay_recv.at[(groups - 1) * group],
        me,
        other,
    )
    own_relay.start()
    read_left.wait()
    read_right.wait()

    def grams(slot):
        def tile(index, carry):
            start = pl.multiple_of(index * depth, depth)
            out_part = pl.ds(start, depth)
            part = pl.ds(pl.multiple_of(core * half + start, depth), depth)
            filled = jnp.full((depth, size), filled_ref[me * cores + slot], jnp.int32) > 0
            left_gram = lax.dot_general(
                gradients[slot, part, :],
                gradients[slot],
                (((1,), (1,)), ((), ())),
                preferred_element_type=jnp.float32,
            )
            left_out[slot, out_part] += jnp.where(filled, left_gram, 0.0)
            right_gram = lax.dot_general(
                gradients[slot, :, part],
                gradients[slot],
                (((0,), (0,)), ((), ())),
                preferred_element_type=jnp.float32,
            )
            right_out[slot, out_part] += jnp.where(filled, right_gram, 0.0)
            return carry

        lax.fori_loop(0, half // depth, tile, 0)

    grams(core)
    give_gradient.wait_recv()
    grams(other)

    def relay(device, index):
        return remote(
            returned_out.at[core, device],
            returned_out.at[core, device],
            relay_send.at[index],
            relay_recv.at[index],
            me,
            other,
        )

    for shift in near_first:
        order = far_first.index(shift)

        def start_relay(step, carry):
            index = order * group + step
            back(me, index).wait_recv()
            relay(origin(shift, step), index).start()
            return carry

        lax.fori_loop(0 if shift else 1, group, start_relay, 0)

    def wait_factor(step, carry):
        give_factor(me, step).wait_recv()
        return carry

    lax.fori_loop(1, owners, wait_factor, 0)
    keep_factor.wait()
    whole_factor = remote(
        factor_out.at[core], factor_out.at[core], whole_send.at[1], whole_recv.at[1], me, other
    )
    whole_factor.start()

    def drain(index, carry):
        swap(me, index).wait_send()
        relay(me, index).wait()
        return carry

    lax.fori_loop(0, owners, drain, 0)

    def drain_far(index, carry):
        there(me, index).wait_send()
        back(me, index).wait_send()
        return carry

    lax.fori_loop(0, (groups - 1) * group, drain_far, 0)
    lax.fori_loop((groups - 1) * group + 1, owners, drain_far, 0)

    def drain_factor(step, carry):
        give_factor(me, step).wait_send()
        return carry

    lax.fori_loop(1, owners, drain_factor, 0)
    give_left.wait_send()
    give_right.wait_send()
    keep_back.wait()
    give_gradient.wait_send()
    whole_factor.wait()


def exchange(source, filled, grads, left_root, right_root, left_stats, right_stats):
    slots, half, size = left_root.shape
    rows = grads.shape[1]
    owners = lax.axis_size("fsdp")
    cores = lax.axis_size("dp")
    group = max(1, min(owners, 256 // rows))
    dma = pltpu.SemaphoreType.DMA
    bf16, f32 = jnp.bfloat16, jnp.float32
    anywhere = pl.BlockSpec(memory_space=pl.ANY)
    inside = pl.BlockSpec(memory_space=pltpu.VMEM)
    scalars = pl.BlockSpec(memory_space=pltpu.SMEM)
    return pl.pallas_call(
        functools.partial(exchange_kernel, (owners, cores, rows, size, group)),
        out_shape=(
            pltpu.VMEM(left_stats.shape, f32),
            pltpu.VMEM(left_stats.shape, f32),
            pltpu.VMEM((cores, owners, rows, size), bf16),
            pltpu.VMEM((cores, owners, 8, 128), f32),
        ),
        in_specs=[scalars] * 2 + [anywhere] * 5,
        out_specs=(inside,) * 4,
        scratch_shapes=[
            pltpu.VMEM((grads.shape[2] // size, rows, size), bf16),
            pltpu.VMEM((owners, rows, size), bf16),
            pltpu.VMEM((owners, rows, size), bf16),
            pltpu.VMEM((owners, rows, size), bf16),
            pltpu.VMEM((cores, size, size), bf16),
            pltpu.VMEM((size, size), bf16),
            pltpu.VMEM((size, size), bf16),
            pltpu.VMEM((size, size), f32),
            pltpu.VMEM((size, size), bf16),
            pltpu.VMEM((8, 128), f32),
            dma,
            dma((2,)),
            dma((3,)),
            dma((2,)),
            dma((2,)),
        ]
        + [dma((owners,))] * 10
        + [dma((2,)), dma((2,))],
        compiler_params=pltpu.CompilerParams(
            collective_id=0, has_side_effects=True, vmem_limit_bytes=VMEM_BYTES
        ),
    )(source, filled, grads, left_root, right_root, left_stats, right_stats)


def finish_kernel(
    steps, slot_ref, left, right, returned, factor, left_out, right_out, update_out, update, sems
):
    cores, size = returned.shape[0], returned.shape[3]
    count = update.shape[1] // size // steps
    copies = [
        pltpu.make_async_copy(left, left_out, sems.at[0]),
        pltpu.make_async_copy(right, right_out, sems.at[1]),
    ]
    copies[0].start()
    copies[1].start()
    for step in range(steps):
        for index in range(step * count, (step + 1) * count):
            slot = slot_ref[index]
            owner, core = slot // cores, slot % cores
            scale = factor[core, owner][:1, :1]
            piece = returned[core, owner].astype(jnp.float32) * scale
            update[:, index * size : (index + 1) * size] = piece.astype(update.dtype)
        columns = pl.ds(step * count * size, count * size)
        copy = pltpu.make_async_copy(
            update.at[:, columns], update_out.at[:, columns], sems.at[2 + step]
        )
        copy.start()
        copies.append(copy)
    for copy in copies:
        copy.wait()


def finish(block_slot, left, right, returned, factor):
    cores, owners, rows, size = returned.shape
    blocks = block_slot.shape[0]
    steps = next(n for n in (4, 2, 1) if blocks % n == 0)
    anywhere = pl.BlockSpec(memory_space=pl.ANY)
    inside = pl.BlockSpec(memory_space=pltpu.VMEM)
    stats = jax.ShapeDtypeStruct(left.shape, left.dtype)
    update = jax.ShapeDtypeStruct((rows, blocks * size), returned.dtype)
    return pl.pallas_call(
        functools.partial(finish_kernel, steps),
        out_shape=(stats, stats, update),
        in_specs=[pl.BlockSpec(memory_space=pltpu.SMEM)] + [inside] * 4,
        out_specs=(anywhere,) * 3,
        scratch_shapes=[
            pltpu.VMEM(update.shape, update.dtype),
            pltpu.SemaphoreType.DMA((2 + steps,)),
        ],
        compiler_params=pltpu.CompilerParams(vmem_limit_bytes=FINISH_BYTES),
    )(block_slot, left, right, returned, factor)


def slot_per_core(grads, block_slot, left_stats, right_stats, left_root, right_root):
    block_count = block_slot.shape[0]
    total_slots = left_stats.shape[0] * lax.axis_size("fsdp")
    matches = block_slot[None, :] == jnp.arange(total_slots, dtype=jnp.int32)[:, None]
    numbers = jnp.arange(block_count, dtype=jnp.int32)
    source = jnp.sum(jnp.where(matches, numbers[None, :], 0), axis=1)
    filled = jnp.sum(matches.astype(jnp.int32), axis=1)
    left, right, returned, factor = exchange(
        source, filled, grads, left_root, right_root, left_stats, right_stats
    )
    return finish(block_slot, left, right, returned, factor)


def per_device(grads, block_slot, left_stats, right_stats, left_root, right_root):
    local_rows = grads[0]
    row_dev, col_count = local_rows.shape
    block_size = left_stats.shape[2]
    block_count = col_count // block_size
    slot_count = left_stats.shape[0]
    shared_rows = left_stats.shape[1]
    total_slots = slot_count * lax.axis_size("fsdp")
    slot_ids = jnp.arange(total_slots, dtype=jnp.int32)
    matches = block_slot[None, :] == slot_ids[:, None]
    filled = jnp.any(matches, axis=1)
    source = jnp.sum(
        jnp.where(matches, jnp.arange(block_count, dtype=jnp.int32)[None, :], 0), axis=1
    )
    row_start = lax.axis_index("dp") * shared_rows
    band = local_rows.astype(jnp.float32).reshape(row_dev, block_count, block_size)
    shares = lax.psum_scatter(band.astype(jnp.bfloat16), "dp", scatter_dimension=2, tiled=True)
    outgoing = jnp.where(
        filled[None, :, None], jnp.take(shares, source, axis=1), jnp.zeros((), jnp.bfloat16)
    )
    incoming = lax.all_to_all(outgoing, "fsdp", split_axis=1, concat_axis=0, tiled=True)
    gradient = lax.all_gather(incoming, "dp", axis=2, tiled=True)
    own_rows = lax.dynamic_slice_in_dim(gradient, row_start, shared_rows, 0)
    whole_right = lax.all_gather(right_root, "dp", axis=1, tiled=True)
    left_new = left_stats + jnp.einsum(
        "rjc,kjc->jrk", own_rows, gradient, preferred_element_type=jnp.float32
    )
    columns = lax.dynamic_slice_in_dim(gradient, row_start, shared_rows, 2)
    right_new = right_stats + jnp.einsum(
        "rjc,rjk->jck", columns, gradient, preferred_element_type=jnp.float32
    )
    left_applied = jnp.einsum(
        "jrk,kjc->rjc", left_root, gradient, preferred_element_type=jnp.float32
    ).astype(jnp.bfloat16)
    both_applied = jnp.einsum(
        "rjc,jck->rjk", left_applied, whole_right, preferred_element_type=jnp.float32
    )
    squares = lax.psum(jnp.sum(both_applied * both_applied, axis=(0, 2)), "dp")
    factor = lax.rsqrt(squares / (block_size * block_size) + epsilon)
    scaled = (both_applied * factor[None, :, None]).astype(jnp.bfloat16)
    full_rows = lax.all_gather(scaled, "dp", axis=0, tiled=True)
    returned = lax.all_to_all(full_rows, "fsdp", split_axis=0, concat_axis=1, tiled=True)
    update = jnp.take(returned, block_slot, axis=1).reshape(row_dev, col_count)
    return (left_new, right_new, update)


def per_shard(*args):
    grads, _, left_stats = args[:3]
    slots, rows = left_stats.shape[0], grads.shape[1]
    paired = slots == 2 and lax.axis_size("dp") == 2
    even = rows % 16 == 0 and 256 % rows == 0 and lax.axis_size("fsdp") % (256 // rows) == 0
    if paired and even:
        return slot_per_core(*args)
    return per_device(*args)


def solution(mesh):
    in_specs = (
        P("dp", "fsdp", None),
        P(),
        P("fsdp", "dp", None),
        P("fsdp", "dp", None),
        P("fsdp", "dp", None),
        P("fsdp", "dp", None),
    )
    out_specs = (P("fsdp", "dp", None), P("fsdp", "dp", None), P("fsdp", None))
    return jax.shard_map(
        per_shard, mesh=mesh, in_specs=in_specs, out_specs=out_specs, check_vma=False
    )
```

```python
import functools
import jax
import jax.numpy as jnp
from jax import lax
from jax.experimental import pallas as pl
from jax.experimental.pallas import tpu as pltpu
from jax.sharding import PartitionSpec as P

epsilon = 1e-06
VMEM_BYTES = 44 * 1024 * 1024
FINISH_BYTES = 28 * 1024 * 1024


def exchange_kernel(
    sizes,
    source_ref,
    filled_ref,
    grads_hbm,
    left_hbm,
    right_hbm,
    left_stats,
    right_stats,
    left_out,
    right_out,
    returned_out,
    factor_out,
    grads,
    outgoing,
    incoming,
    summed,
    gradients,
    left,
    right,
    total,
    applied,
    factor,
    load_sem,
    stats_sem,
    local_sem,
    root_send,
    root_recv,
    swap_send,
    swap_recv,
    there_send,
    there_recv,
    back_send,
    back_recv,
    relay_send,
    relay_recv,
    factor_send,
    factor_recv,
    whole_send,
    whole_recv,
):
    owners, cores, rows, size, group = sizes
    groups = owners // group
    depth = group * rows
    half = size // cores
    me = lax.axis_index("fsdp")
    core = lax.axis_index("dp")
    other = 1 - core
    gradient = gradients.at[core]
    my_group = me // group
    my_place = me % group
    far_first = [groups // 2] + [d for d in range(1, groups) if d != groups // 2] + [0]
    near_first = [0] + far_first[:-1]

    def flipped(value, mask, count):
        result, bit = 0, 1
        while bit < count:
            result = result + bit * ((value // bit + mask // bit) % 2)
            bit = 2 * bit
        return result

    def target(shift, step):
        return flipped(my_group, shift, groups) * group + flipped(my_place, step, group)

    def block_rows(device):
        return pl.ds(pl.multiple_of(device * rows, rows), rows)

    def chosen(slot):
        return grads[source_ref[slot]]

    def remote(src, dst, send, recv, owner, to_core):
        return pltpu.make_async_remote_copy(
            src_ref=src,
            dst_ref=dst,
            send_sem=send,
            recv_sem=recv,
            device_id={"fsdp": owner, "dp": to_core},
            device_id_type=pl.DeviceIdType.MESH,
        )

    def load(block, carry):
        columns = pl.ds(pl.multiple_of(block * size, size), size)
        pltpu.make_async_copy(grads_hbm.at[0, :, columns], grads.at[block], load_sem).start()
        return carry

    lax.fori_loop(0, grads.shape[0], load, 0)
    barrier = pltpu.get_barrier_semaphore()
    pl.semaphore_signal(
        barrier,
        inc=1,
        device_id={"fsdp": me, "dp": other},
        device_id_type=pl.DeviceIdType.MESH,
    )

    def greet(step, carry):
        pl.semaphore_signal(
            barrier,
            inc=1,
            device_id={"fsdp": (me + step) % owners, "dp": core},
            device_id_type=pl.DeviceIdType.MESH,
        )
        return carry

    lax.fori_loop(1, owners, greet, 0)
    own_half = pl.ds(pl.multiple_of(core * half, half), half)
    other_half = pl.ds(pl.multiple_of(other * half, half), half)
    keep_left = pltpu.make_async_copy(left_hbm.at[core], left.at[own_half], local_sem.at[0])
    keep_right = pltpu.make_async_copy(right_hbm.at[core], right.at[own_half], local_sem.at[1])
    keep_left.start()
    keep_right.start()
    read_left = pltpu.make_async_copy(left_stats, left_out, stats_sem.at[0])
    read_right = pltpu.make_async_copy(right_stats, right_out, stats_sem.at[1])
    read_left.start()
    read_right.start()
    pltpu.make_async_copy(grads, grads, load_sem).wait()

    def pick(device, carry):
        outgoing[device] = chosen(device * cores + other)
        return carry

    lax.fori_loop(0, owners, pick, 0)
    pl.semaphore_wait(barrier, owners)

    def swap(device, index):
        return remote(
            outgoing.at[device],
            incoming.at[device],
            swap_send.at[index],
            swap_recv.at[index],
            me,
            other,
        )

    for order, shift in enumerate(far_first):

        def start_swap(step, carry):
            swap(target(shift, step), order * group + step).start()
            return carry

        lax.fori_loop(0, group, start_swap, 0)

    give_left = remote(
        left_hbm.at[other], left.at[own_half], root_send.at[0], root_recv.at[0], me, other
    )
    give_right = remote(
        right_hbm.at[other], right.at[own_half], root_send.at[1], root_recv.at[1], me, other
    )
    give_left.start()
    give_right.start()

    def there(device, index):
        return remote(
            summed.at[device],
            gradient.at[block_rows(me)],
            there_send.at[index],
            there_recv.at[index],
            device,
            core,
        )

    def summed_block(device, index):
        mine = chosen(device * cores + core)
        swap(device, index).wait_recv()
        return (mine.astype(jnp.float32) + incoming[device].astype(jnp.float32)).astype(
            jnp.bfloat16
        )

    for order, shift in enumerate(far_first):

        def start_there(step, carry):
            device = target(shift, step)
            index = order * group + step
            summed[device] = summed_block(device, index)
            there(device, index).start()
            return carry

        lax.fori_loop(0 if shift else 1, group, start_there, 0)
    gradient[block_rows(me)] = summed_block(me, (groups - 1) * group)

    keep_left.wait()
    keep_right.wait()
    give_left.wait_recv()
    give_right.wait_recv()

    def wait_there(shift):
        order = far_first.index(shift)

        def body(step, carry):
            there(me, order * group + step).wait_recv()
            return carry

        lax.fori_loop(0 if shift else 1, group, body, 0)

    def group_rows(index):
        return pl.ds(pl.multiple_of(index * depth, depth), depth)

    for order, shift in enumerate(near_first[:-1]):
        wait_there(shift)
        deep = group_rows(flipped(my_group, shift, groups))

        def accumulate(index, carry):
            part = jnp.dot(
                left[group_rows(index), deep],
                gradient[deep],
                preferred_element_type=jnp.float32,
            )
            if order:
                part = part + total[group_rows(index)]
            total[group_rows(index)] = part
            return carry

        lax.fori_loop(0, groups, accumulate, 0)

    wait_there(near_first[-1])
    deep = group_rows(flipped(my_group, near_first[-1], groups))

    def back(device, index):
        return remote(
            applied.at[block_rows(device)],
            returned_out.at[core, me],
            back_send.at[index],
            back_recv.at[index],
            device,
            core,
        )

    give_gradient = remote(gradient, gradient, whole_send.at[0], whole_recv.at[0], me, other)
    give_gradient.start()
    squares = jnp.zeros((1, size), jnp.float32)
    for order, shift in enumerate(far_first):
        out_rows = group_rows(flipped(my_group, shift, groups))
        left_applied = jnp.dot(
            left[out_rows, deep], gradient[deep], preferred_element_type=jnp.float32
        )
        left_applied = (left_applied + total[out_rows]).astype(jnp.bfloat16)
        both = jnp.dot(left_applied, right[...], preferred_element_type=jnp.float32)
        squares = squares + jnp.sum(both * both, axis=0, keepdims=True)
        applied[out_rows] = both.astype(jnp.bfloat16)

        def start_back(step, carry):
            back(target(shift, step), order * group + step).start()
            return carry

        lax.fori_loop(0 if shift else 1, group, start_back, 0)

    scale = lax.rsqrt(jnp.sum(squares, axis=1, keepdims=True) / (size * size) + epsilon)
    factor[...] = jnp.broadcast_to(scale, factor.shape)

    def give_factor(device, index):
        return remote(
            factor,
            factor_out.at[core, me],
            factor_send.at[index],
            factor_recv.at[index],
            device,
            core,
        )

    def start_factor(step, carry):
        give_factor((me + step) % owners, step).start()
        return carry

    lax.fori_loop(1, owners, start_factor, 0)
    keep_factor = pltpu.make_async_copy(factor, factor_out.at[core, me], local_sem.at[0])
    keep_factor.start()
    keep_back = pltpu.make_async_copy(
        applied.at[block_rows(me)], returned_out.at[core, me], local_sem.at[2]
    )
    keep_back.start()
    own_relay = remote(
        applied.at[block_rows(me)],
        returned_out.at[core, me],
        relay_send.at[(groups - 1) * group],
        relay_recv.at[(groups - 1) * group],
        me,
        other,
    )
    own_relay.start()
    read_left.wait()
    read_right.wait()

    def grams(slot):
        def tile(index, carry):
            start = pl.multiple_of(index * depth, depth)
            out_part = pl.ds(start, depth)
            part = pl.ds(pl.multiple_of(core * half + start, depth), depth)
            filled = jnp.full((depth, size), filled_ref[me * cores + slot], jnp.int32) > 0
            left_gram = lax.dot_general(
                gradients[slot, part, :],
                gradients[slot],
                (((1,), (1,)), ((), ())),
                preferred_element_type=jnp.float32,
            )
            left_out[slot, out_part] += jnp.where(filled, left_gram, 0.0)
            right_gram = lax.dot_general(
                gradients[slot, :, part],
                gradients[slot],
                (((0,), (0,)), ((), ())),
                preferred_element_type=jnp.float32,
            )
            right_out[slot, out_part] += jnp.where(filled, right_gram, 0.0)
            return carry

        lax.fori_loop(0, half // depth, tile, 0)

    grams(core)
    give_gradient.wait_recv()
    grams(other)

    def relay(device, index):
        return remote(
            returned_out.at[core, device],
            returned_out.at[core, device],
            relay_send.at[index],
            relay_recv.at[index],
            me,
            other,
        )

    for shift in near_first:
        order = far_first.index(shift)

        def start_relay(step, carry):
            index = order * group + step
            back(me, index).wait_recv()
            relay(target(shift, step), index).start()
            return carry

        lax.fori_loop(0 if shift else 1, group, start_relay, 0)

    def wait_factor(step, carry):
        give_factor(me, step).wait_recv()
        return carry

    lax.fori_loop(1, owners, wait_factor, 0)
    keep_factor.wait()
    whole_factor = remote(
        factor_out.at[core], factor_out.at[core], whole_send.at[1], whole_recv.at[1], me, other
    )
    whole_factor.start()

    def drain(index, carry):
        swap(me, index).wait_send()
        relay(me, index).wait()
        return carry

    lax.fori_loop(0, owners, drain, 0)

    def drain_far(index, carry):
        there(me, index).wait_send()
        back(me, index).wait_send()
        return carry

    lax.fori_loop(0, (groups - 1) * group, drain_far, 0)
    lax.fori_loop((groups - 1) * group + 1, owners, drain_far, 0)

    def drain_factor(step, carry):
        give_factor(me, step).wait_send()
        return carry

    lax.fori_loop(1, owners, drain_factor, 0)
    give_left.wait_send()
    give_right.wait_send()
    keep_back.wait()
    give_gradient.wait_send()
    whole_factor.wait()


def exchange(source, filled, grads, left_root, right_root, left_stats, right_stats):
    slots, half, size = left_root.shape
    rows = grads.shape[1]
    owners = lax.axis_size("fsdp")
    cores = lax.axis_size("dp")
    group = max(1, min(owners, 256 // rows))
    dma = pltpu.SemaphoreType.DMA
    bf16, f32 = jnp.bfloat16, jnp.float32
    anywhere = pl.BlockSpec(memory_space=pl.ANY)
    inside = pl.BlockSpec(memory_space=pltpu.VMEM)
    scalars = pl.BlockSpec(memory_space=pltpu.SMEM)
    return pl.pallas_call(
        functools.partial(exchange_kernel, (owners, cores, rows, size, group)),
        out_shape=(
            pltpu.VMEM(left_stats.shape, f32),
            pltpu.VMEM(left_stats.shape, f32),
            pltpu.VMEM((cores, owners, rows, size), bf16),
            pltpu.VMEM((cores, owners, 8, 128), f32),
        ),
        in_specs=[scalars] * 2 + [anywhere] * 5,
        out_specs=(inside,) * 4,
        scratch_shapes=[
            pltpu.VMEM((grads.shape[2] // size, rows, size), bf16),
            pltpu.VMEM((owners, rows, size), bf16),
            pltpu.VMEM((owners, rows, size), bf16),
            pltpu.VMEM((owners, rows, size), bf16),
            pltpu.VMEM((cores, size, size), bf16),
            pltpu.VMEM((size, size), bf16),
            pltpu.VMEM((size, size), bf16),
            pltpu.VMEM((size, size), f32),
            pltpu.VMEM((size, size), bf16),
            pltpu.VMEM((8, 128), f32),
            dma,
            dma((2,)),
            dma((3,)),
            dma((2,)),
            dma((2,)),
        ]
        + [dma((owners,))] * 10
        + [dma((2,)), dma((2,))],
        compiler_params=pltpu.CompilerParams(
            collective_id=0, has_side_effects=True, vmem_limit_bytes=VMEM_BYTES
        ),
    )(source, filled, grads, left_root, right_root, left_stats, right_stats)


def finish_kernel(
    steps, slot_ref, left, right, returned, factor, left_out, right_out, update_out, update, sems
):
    cores, size = returned.shape[0], returned.shape[3]
    count = update.shape[1] // size // steps
    copies = [
        pltpu.make_async_copy(left, left_out, sems.at[0]),
        pltpu.make_async_copy(right, right_out, sems.at[1]),
    ]
    copies[0].start()
    copies[1].start()
    for step in range(steps):
        for index in range(step * count, (step + 1) * count):
            slot = slot_ref[index]
            owner, core = slot // cores, slot % cores
            scale = factor[core, owner][:1, :1]
            piece = returned[core, owner].astype(jnp.float32) * scale
            update[:, index * size : (index + 1) * size] = piece.astype(update.dtype)
        columns = pl.ds(step * count * size, count * size)
        copy = pltpu.make_async_copy(
            update.at[:, columns], update_out.at[:, columns], sems.at[2 + step]
        )
        copy.start()
        copies.append(copy)
    for copy in copies:
        copy.wait()


def finish(block_slot, left, right, returned, factor):
    cores, owners, rows, size = returned.shape
    blocks = block_slot.shape[0]
    steps = next(n for n in (4, 2, 1) if blocks % n == 0)
    anywhere = pl.BlockSpec(memory_space=pl.ANY)
    inside = pl.BlockSpec(memory_space=pltpu.VMEM)
    stats = jax.ShapeDtypeStruct(left.shape, left.dtype)
    update = jax.ShapeDtypeStruct((rows, blocks * size), returned.dtype)
    return pl.pallas_call(
        functools.partial(finish_kernel, steps),
        out_shape=(stats, stats, update),
        in_specs=[pl.BlockSpec(memory_space=pltpu.SMEM)] + [inside] * 4,
        out_specs=(anywhere,) * 3,
        scratch_shapes=[
            pltpu.VMEM(update.shape, update.dtype),
            pltpu.SemaphoreType.DMA((2 + steps,)),
        ],
        compiler_params=pltpu.CompilerParams(vmem_limit_bytes=FINISH_BYTES),
    )(block_slot, left, right, returned, factor)


def slot_per_core(grads, block_slot, left_stats, right_stats, left_root, right_root):
    block_count = block_slot.shape[0]
    total_slots = left_stats.shape[0] * lax.axis_size("fsdp")
    matches = block_slot[None, :] == jnp.arange(total_slots, dtype=jnp.int32)[:, None]
    numbers = jnp.arange(block_count, dtype=jnp.int32)
    source = jnp.sum(jnp.where(matches, numbers[None, :], 0), axis=1)
    filled = jnp.sum(matches.astype(jnp.int32), axis=1)
    left, right, returned, factor = exchange(
        source, filled, grads, left_root, right_root, left_stats, right_stats
    )
    return finish(block_slot, left, right, returned, factor)


def per_device(grads, block_slot, left_stats, right_stats, left_root, right_root):
    local_rows = grads[0]
    row_dev, col_count = local_rows.shape
    block_size = left_stats.shape[2]
    block_count = col_count // block_size
    slot_count = left_stats.shape[0]
    shared_rows = left_stats.shape[1]
    total_slots = slot_count * lax.axis_size("fsdp")
    slot_ids = jnp.arange(total_slots, dtype=jnp.int32)
    matches = block_slot[None, :] == slot_ids[:, None]
    filled = jnp.any(matches, axis=1)
    source = jnp.sum(
        jnp.where(matches, jnp.arange(block_count, dtype=jnp.int32)[None, :], 0), axis=1
    )
    row_start = lax.axis_index("dp") * shared_rows
    band = local_rows.astype(jnp.float32).reshape(row_dev, block_count, block_size)
    shares = lax.psum_scatter(band.astype(jnp.bfloat16), "dp", scatter_dimension=2, tiled=True)
    outgoing = jnp.where(
        filled[None, :, None], jnp.take(shares, source, axis=1), jnp.zeros((), jnp.bfloat16)
    )
    incoming = lax.all_to_all(outgoing, "fsdp", split_axis=1, concat_axis=0, tiled=True)
    gradient = lax.all_gather(incoming, "dp", axis=2, tiled=True)
    own_rows = lax.dynamic_slice_in_dim(gradient, row_start, shared_rows, 0)
    whole_right = lax.all_gather(right_root, "dp", axis=1, tiled=True)
    left_new = left_stats + jnp.einsum(
        "rjc,kjc->jrk", own_rows, gradient, preferred_element_type=jnp.float32
    )
    columns = lax.dynamic_slice_in_dim(gradient, row_start, shared_rows, 2)
    right_new = right_stats + jnp.einsum(
        "rjc,rjk->jck", columns, gradient, preferred_element_type=jnp.float32
    )
    left_applied = jnp.einsum(
        "jrk,kjc->rjc", left_root, gradient, preferred_element_type=jnp.float32
    ).astype(jnp.bfloat16)
    both_applied = jnp.einsum(
        "rjc,jck->rjk", left_applied, whole_right, preferred_element_type=jnp.float32
    )
    squares = lax.psum(jnp.sum(both_applied * both_applied, axis=(0, 2)), "dp")
    factor = lax.rsqrt(squares / (block_size * block_size) + epsilon)
    scaled = (both_applied * factor[None, :, None]).astype(jnp.bfloat16)
    full_rows = lax.all_gather(scaled, "dp", axis=0, tiled=True)
    returned = lax.all_to_all(full_rows, "fsdp", split_axis=0, concat_axis=1, tiled=True)
    update = jnp.take(returned, block_slot, axis=1).reshape(row_dev, col_count)
    return (left_new, right_new, update)


def per_shard(*args):
    grads, _, left_stats = args[:3]
    slots, rows = left_stats.shape[0], grads.shape[1]
    paired = slots == 2 and lax.axis_size("dp") == 2
    even = rows % 16 == 0 and 256 % rows == 0 and lax.axis_size("fsdp") % (256 // rows) == 0
    if paired and even and lax.axis_size("fsdp").bit_count() == 1:
        return slot_per_core(*args)
    return per_device(*args)


def solution(mesh):
    in_specs = (
        P("dp", "fsdp", None),
        P(),
        P("fsdp", "dp", None),
        P("fsdp", "dp", None),
        P("fsdp", "dp", None),
        P("fsdp", "dp", None),
    )
    out_specs = (P("fsdp", "dp", None), P("fsdp", "dp", None), P("fsdp", None))
    return jax.shard_map(
        per_shard, mesh=mesh, in_specs=in_specs, out_specs=out_specs, check_vma=False
    )
```

```python
import functools
import jax
import jax.numpy as jnp
from jax import lax
from jax.experimental import pallas as pl
from jax.experimental.pallas import tpu as pltpu
from jax.sharding import PartitionSpec as P

epsilon = 1e-06
VMEM_BYTES = 44 * 1024 * 1024
FINISH_BYTES = 28 * 1024 * 1024


def exchange_kernel(
    sizes,
    source_ref,
    filled_ref,
    grads_hbm,
    left_hbm,
    right_hbm,
    left_stats,
    right_stats,
    left_out,
    right_out,
    returned_out,
    factor_out,
    grads,
    outgoing,
    incoming,
    summed,
    gradients,
    left,
    right,
    total,
    applied,
    factor,
    load_sem,
    stats_sem,
    local_sem,
    root_send,
    root_recv,
    swap_send,
    swap_recv,
    there_send,
    there_recv,
    back_send,
    back_recv,
    relay_send,
    relay_recv,
    factor_send,
    factor_recv,
    whole_send,
    whole_recv,
):
    owners, cores, rows, size, group = sizes
    groups = owners // group
    depth = group * rows
    half = size // cores
    me = lax.axis_index("fsdp")
    core = lax.axis_index("dp")
    other = 1 - core
    gradient = gradients.at[core]
    my_group = me // group
    my_place = me % group
    far_first = [groups // 2] + [d for d in range(groups - 1, 0, -1) if d != groups // 2] + [0]
    near_first = [0] + far_first[:-1]

    def target(shift, step):
        return ((my_group + shift) % groups) * group + (my_place + step) % group

    def origin(shift, step):
        return ((my_group + groups - shift) % groups) * group + (my_place + group - step) % group

    def block_rows(device):
        return pl.ds(pl.multiple_of(device * rows, rows), rows)

    def chosen(slot):
        return grads[source_ref[slot]]

    def remote(src, dst, send, recv, owner, to_core):
        return pltpu.make_async_remote_copy(
            src_ref=src,
            dst_ref=dst,
            send_sem=send,
            recv_sem=recv,
            device_id={"fsdp": owner, "dp": to_core},
            device_id_type=pl.DeviceIdType.MESH,
        )

    barrier = pltpu.get_barrier_semaphore()
    pl.semaphore_signal(
        barrier,
        inc=1,
        device_id={"fsdp": me, "dp": other},
        device_id_type=pl.DeviceIdType.MESH,
    )

    def greet(step, carry):
        pl.semaphore_signal(
            barrier,
            inc=1,
            device_id={"fsdp": (me + step) % owners, "dp": core},
            device_id_type=pl.DeviceIdType.MESH,
        )
        return carry

    lax.fori_loop(1, owners, greet, 0)

    def load(block, carry):
        columns = pl.ds(pl.multiple_of(block * size, size), size)
        pltpu.make_async_copy(grads_hbm.at[0, :, columns], grads.at[block], load_sem).start()
        return carry

    lax.fori_loop(0, grads.shape[0], load, 0)
    own_half = pl.ds(pl.multiple_of(core * half, half), half)
    other_half = pl.ds(pl.multiple_of(other * half, half), half)
    keep_left = pltpu.make_async_copy(left_hbm.at[core], left.at[own_half], local_sem.at[0])
    keep_right = pltpu.make_async_copy(right_hbm.at[core], right.at[own_half], local_sem.at[1])
    pltpu.make_async_copy(grads, grads, load_sem).wait()

    def pick(device, carry):
        outgoing[device] = chosen(device * cores + other)
        return carry

    lax.fori_loop(0, owners, pick, 0)
    pl.semaphore_wait(barrier, owners)

    def swap(device, index):
        return remote(
            outgoing.at[device],
            incoming.at[device],
            swap_send.at[index],
            swap_recv.at[index],
            me,
            other,
        )

    for order, shift in enumerate(far_first):

        def start_swap(step, carry):
            swap(target(shift, step), order * group + step).start()
            return carry

        lax.fori_loop(0, group, start_swap, 0)

    give_left = remote(
        left_hbm.at[other], left.at[own_half], root_send.at[0], root_recv.at[0], me, other
    )
    give_right = remote(
        right_hbm.at[other], right.at[own_half], root_send.at[1], root_recv.at[1], me, other
    )
    give_left.start()
    give_right.start()
    keep_left.start()
    keep_right.start()

    def there(device, index):
        return remote(
            summed.at[device],
            gradient.at[block_rows(me)],
            there_send.at[index],
            there_recv.at[index],
            device,
            core,
        )

    def summed_block(device, index):
        mine = chosen(device * cores + core)
        swap(device, index).wait_recv()
        return (mine.astype(jnp.float32) + incoming[device].astype(jnp.float32)).astype(
            jnp.bfloat16
        )

    for order, shift in enumerate(far_first):

        def start_there(step, carry):
            device = target(shift, step)
            index = order * group + step
            summed[device] = summed_block(device, index)
            there(device, index).start()
            return carry

        lax.fori_loop(0 if shift else 1, group, start_there, 0)
    read_left = pltpu.make_async_copy(left_stats, left_out, stats_sem.at[0])
    read_right = pltpu.make_async_copy(right_stats, right_out, stats_sem.at[1])
    read_left.start()
    read_right.start()
    gradient[block_rows(me)] = summed_block(me, (groups - 1) * group)

    keep_left.wait()
    keep_right.wait()
    give_left.wait_recv()
    give_right.wait_recv()

    def wait_there(shift):
        order = far_first.index(shift)

        def body(step, carry):
            there(me, order * group + step).wait_recv()
            return carry

        lax.fori_loop(0 if shift else 1, group, body, 0)

    def group_rows(index):
        return pl.ds(pl.multiple_of(index * depth, depth), depth)

    for order, shift in enumerate(near_first[:-1]):
        wait_there(shift)
        deep = group_rows((my_group + groups - shift) % groups)

        def accumulate(index, carry):
            part = jnp.dot(
                left[group_rows(index), deep],
                gradient[deep],
                preferred_element_type=jnp.float32,
            )
            if order:
                part = part + total[group_rows(index)]
            total[group_rows(index)] = part
            return carry

        lax.fori_loop(0, groups, accumulate, 0)

    wait_there(near_first[-1])
    deep = group_rows((my_group + groups - near_first[-1]) % groups)

    def back(device, index):
        return remote(
            applied.at[block_rows(device)],
            returned_out.at[core, me],
            back_send.at[index],
            back_recv.at[index],
            device,
            core,
        )

    give_gradient = remote(gradient, gradient, whole_send.at[0], whole_recv.at[0], me, other)
    give_gradient.start()
    squares = jnp.zeros((1, size), jnp.float32)
    for order, shift in enumerate(far_first):
        out_rows = group_rows((my_group + shift) % groups)
        left_applied = jnp.dot(
            left[out_rows, deep], gradient[deep], preferred_element_type=jnp.float32
        )
        left_applied = (left_applied + total[out_rows]).astype(jnp.bfloat16)
        both = jnp.dot(left_applied, right[...], preferred_element_type=jnp.float32)
        squares = squares + jnp.sum(both * both, axis=0, keepdims=True)
        applied[out_rows] = both.astype(jnp.bfloat16)

        def start_back(step, carry):
            back(target(shift, step), order * group + step).start()
            return carry

        lax.fori_loop(0 if shift else 1, group, start_back, 0)

    scale = lax.rsqrt(jnp.sum(squares, axis=1, keepdims=True) / (size * size) + epsilon)
    factor[...] = jnp.broadcast_to(scale, factor.shape)

    def give_factor(device, index):
        return remote(
            factor,
            factor_out.at[core, me],
            factor_send.at[index],
            factor_recv.at[index],
            device,
            core,
        )

    def start_factor(step, carry):
        give_factor((me + step) % owners, step).start()
        return carry

    lax.fori_loop(1, owners, start_factor, 0)
    keep_factor = pltpu.make_async_copy(factor, factor_out.at[core, me], local_sem.at[0])
    keep_factor.start()
    keep_back = pltpu.make_async_copy(
        applied.at[block_rows(me)], returned_out.at[core, me], local_sem.at[2]
    )
    keep_back.start()
    own_relay = remote(
        applied.at[block_rows(me)],
        returned_out.at[core, me],
        relay_send.at[(groups - 1) * group],
        relay_recv.at[(groups - 1) * group],
        me,
        other,
    )
    own_relay.start()
    read_left.wait()
    read_right.wait()

    def grams(slot):
        def tile(index, carry):
            start = pl.multiple_of(index * depth, depth)
            out_part = pl.ds(start, depth)
            part = pl.ds(pl.multiple_of(core * half + start, depth), depth)
            filled = jnp.full((depth, size), filled_ref[me * cores + slot], jnp.int32) > 0
            left_gram = lax.dot_general(
                gradients[slot, part, :],
                gradients[slot],
                (((1,), (1,)), ((), ())),
                preferred_element_type=jnp.float32,
            )
            left_out[slot, out_part] += jnp.where(filled, left_gram, 0.0)
            right_gram = lax.dot_general(
                gradients[slot, :, part],
                gradients[slot],
                (((0,), (0,)), ((), ())),
                preferred_element_type=jnp.float32,
            )
            right_out[slot, out_part] += jnp.where(filled, right_gram, 0.0)
            return carry

        lax.fori_loop(0, half // depth, tile, 0)

    grams(core)
    give_gradient.wait_recv()
    grams(other)

    def relay(device, index):
        return remote(
            returned_out.at[core, device],
            returned_out.at[core, device],
            relay_send.at[index],
            relay_recv.at[index],
            me,
            other,
        )

    for shift in near_first:
        order = far_first.index(shift)

        def start_relay(step, carry):
            index = order * group + step
            back(me, index).wait_recv()
            relay(origin(shift, step), index).start()
            return carry

        lax.fori_loop(0 if shift else 1, group, start_relay, 0)

    def wait_factor(step, carry):
        give_factor(me, step).wait_recv()
        return carry

    lax.fori_loop(1, owners, wait_factor, 0)
    keep_factor.wait()
    whole_factor = remote(
        factor_out.at[core], factor_out.at[core], whole_send.at[1], whole_recv.at[1], me, other
    )
    whole_factor.start()

    def drain(index, carry):
        swap(me, index).wait_send()
        relay(me, index).wait()
        return carry

    lax.fori_loop(0, owners, drain, 0)

    def drain_far(index, carry):
        there(me, index).wait_send()
        back(me, index).wait_send()
        return carry

    lax.fori_loop(0, (groups - 1) * group, drain_far, 0)
    lax.fori_loop((groups - 1) * group + 1, owners, drain_far, 0)

    def drain_factor(step, carry):
        give_factor(me, step).wait_send()
        return carry

    lax.fori_loop(1, owners, drain_factor, 0)
    give_left.wait_send()
    give_right.wait_send()
    keep_back.wait()
    give_gradient.wait_send()
    whole_factor.wait()


def exchange(source, filled, grads, left_root, right_root, left_stats, right_stats):
    slots, half, size = left_root.shape
    rows = grads.shape[1]
    owners = lax.axis_size("fsdp")
    cores = lax.axis_size("dp")
    group = max(1, min(owners, 256 // rows))
    dma = pltpu.SemaphoreType.DMA
    bf16, f32 = jnp.bfloat16, jnp.float32
    anywhere = pl.BlockSpec(memory_space=pl.ANY)
    inside = pl.BlockSpec(memory_space=pltpu.VMEM)
    scalars = pl.BlockSpec(memory_space=pltpu.SMEM)
    return pl.pallas_call(
        functools.partial(exchange_kernel, (owners, cores, rows, size, group)),
        out_shape=(
            pltpu.VMEM(left_stats.shape, f32),
            pltpu.VMEM(left_stats.shape, f32),
            pltpu.VMEM((cores, owners, rows, size), bf16),
            pltpu.VMEM((cores, owners, 8, 128), f32),
        ),
        in_specs=[scalars] * 2 + [anywhere] * 5,
        out_specs=(inside,) * 4,
        scratch_shapes=[
            pltpu.VMEM((grads.shape[2] // size, rows, size), bf16),
            pltpu.VMEM((owners, rows, size), bf16),
            pltpu.VMEM((owners, rows, size), bf16),
            pltpu.VMEM((owners, rows, size), bf16),
            pltpu.VMEM((cores, size, size), bf16),
            pltpu.VMEM((size, size), bf16),
            pltpu.VMEM((size, size), bf16),
            pltpu.VMEM((size, size), f32),
            pltpu.VMEM((size, size), bf16),
            pltpu.VMEM((8, 128), f32),
            dma,
            dma((2,)),
            dma((3,)),
            dma((2,)),
            dma((2,)),
        ]
        + [dma((owners,))] * 10
        + [dma((2,)), dma((2,))],
        compiler_params=pltpu.CompilerParams(
            collective_id=0, has_side_effects=True, vmem_limit_bytes=VMEM_BYTES
        ),
    )(source, filled, grads, left_root, right_root, left_stats, right_stats)


def finish_kernel(
    steps, slot_ref, left, right, returned, factor, left_out, right_out, update_out, update, sems
):
    cores, size = returned.shape[0], returned.shape[3]
    count = update.shape[1] // size // steps
    copies = [
        pltpu.make_async_copy(left, left_out, sems.at[0]),
        pltpu.make_async_copy(right, right_out, sems.at[1]),
    ]
    copies[0].start()
    copies[1].start()
    for step in range(steps):
        for index in range(step * count, (step + 1) * count):
            slot = slot_ref[index]
            owner, core = slot // cores, slot % cores
            scale = factor[core, owner][:1, :1]
            piece = returned[core, owner].astype(jnp.float32) * scale
            update[:, index * size : (index + 1) * size] = piece.astype(update.dtype)
        columns = pl.ds(step * count * size, count * size)
        copy = pltpu.make_async_copy(
            update.at[:, columns], update_out.at[:, columns], sems.at[2 + step]
        )
        copy.start()
        copies.append(copy)
    for copy in copies:
        copy.wait()


def finish(block_slot, left, right, returned, factor):
    cores, owners, rows, size = returned.shape
    blocks = block_slot.shape[0]
    steps = next(n for n in (4, 2, 1) if blocks % n == 0)
    anywhere = pl.BlockSpec(memory_space=pl.ANY)
    inside = pl.BlockSpec(memory_space=pltpu.VMEM)
    stats = jax.ShapeDtypeStruct(left.shape, left.dtype)
    update = jax.ShapeDtypeStruct((rows, blocks * size), returned.dtype)
    return pl.pallas_call(
        functools.partial(finish_kernel, steps),
        out_shape=(stats, stats, update),
        in_specs=[pl.BlockSpec(memory_space=pltpu.SMEM)] + [inside] * 4,
        out_specs=(anywhere,) * 3,
        scratch_shapes=[
            pltpu.VMEM(update.shape, update.dtype),
            pltpu.SemaphoreType.DMA((2 + steps,)),
        ],
        compiler_params=pltpu.CompilerParams(vmem_limit_bytes=FINISH_BYTES),
    )(block_slot, left, right, returned, factor)


def slot_per_core(grads, block_slot, left_stats, right_stats, left_root, right_root):
    block_count = block_slot.shape[0]
    total_slots = left_stats.shape[0] * lax.axis_size("fsdp")
    matches = block_slot[None, :] == jnp.arange(total_slots, dtype=jnp.int32)[:, None]
    numbers = jnp.arange(block_count, dtype=jnp.int32)
    source = jnp.sum(jnp.where(matches, numbers[None, :], 0), axis=1)
    filled = jnp.sum(matches.astype(jnp.int32), axis=1)
    left, right, returned, factor = exchange(
        source, filled, grads, left_root, right_root, left_stats, right_stats
    )
    return finish(block_slot, left, right, returned, factor)


def per_device(grads, block_slot, left_stats, right_stats, left_root, right_root):
    local_rows = grads[0]
    row_dev, col_count = local_rows.shape
    block_size = left_stats.shape[2]
    block_count = col_count // block_size
    slot_count = left_stats.shape[0]
    shared_rows = left_stats.shape[1]
    total_slots = slot_count * lax.axis_size("fsdp")
    slot_ids = jnp.arange(total_slots, dtype=jnp.int32)
    matches = block_slot[None, :] == slot_ids[:, None]
    filled = jnp.any(matches, axis=1)
    source = jnp.sum(
        jnp.where(matches, jnp.arange(block_count, dtype=jnp.int32)[None, :], 0), axis=1
    )
    row_start = lax.axis_index("dp") * shared_rows
    band = local_rows.astype(jnp.float32).reshape(row_dev, block_count, block_size)
    shares = lax.psum_scatter(band.astype(jnp.bfloat16), "dp", scatter_dimension=2, tiled=True)
    outgoing = jnp.where(
        filled[None, :, None], jnp.take(shares, source, axis=1), jnp.zeros((), jnp.bfloat16)
    )
    incoming = lax.all_to_all(outgoing, "fsdp", split_axis=1, concat_axis=0, tiled=True)
    gradient = lax.all_gather(incoming, "dp", axis=2, tiled=True)
    own_rows = lax.dynamic_slice_in_dim(gradient, row_start, shared_rows, 0)
    whole_right = lax.all_gather(right_root, "dp", axis=1, tiled=True)
    left_new = left_stats + jnp.einsum(
        "rjc,kjc->jrk", own_rows, gradient, preferred_element_type=jnp.float32
    )
    columns = lax.dynamic_slice_in_dim(gradient, row_start, shared_rows, 2)
    right_new = right_stats + jnp.einsum(
        "rjc,rjk->jck", columns, gradient, preferred_element_type=jnp.float32
    )
    left_applied = jnp.einsum(
        "jrk,kjc->rjc", left_root, gradient, preferred_element_type=jnp.float32
    ).astype(jnp.bfloat16)
    both_applied = jnp.einsum(
        "rjc,jck->rjk", left_applied, whole_right, preferred_element_type=jnp.float32
    )
    squares = lax.psum(jnp.sum(both_applied * both_applied, axis=(0, 2)), "dp")
    factor = lax.rsqrt(squares / (block_size * block_size) + epsilon)
    scaled = (both_applied * factor[None, :, None]).astype(jnp.bfloat16)
    full_rows = lax.all_gather(scaled, "dp", axis=0, tiled=True)
    returned = lax.all_to_all(full_rows, "fsdp", split_axis=0, concat_axis=1, tiled=True)
    update = jnp.take(returned, block_slot, axis=1).reshape(row_dev, col_count)
    return (left_new, right_new, update)


def per_shard(*args):
    grads, _, left_stats = args[:3]
    slots, rows = left_stats.shape[0], grads.shape[1]
    paired = slots == 2 and lax.axis_size("dp") == 2
    even = rows % 16 == 0 and 256 % rows == 0 and lax.axis_size("fsdp") % (256 // rows) == 0
    if paired and even:
        return slot_per_core(*args)
    return per_device(*args)


def solution(mesh):
    in_specs = (
        P("dp", "fsdp", None),
        P(),
        P("fsdp", "dp", None),
        P("fsdp", "dp", None),
        P("fsdp", "dp", None),
        P("fsdp", "dp", None),
    )
    out_specs = (P("fsdp", "dp", None), P("fsdp", "dp", None), P("fsdp", None))
    return jax.shard_map(
        per_shard, mesh=mesh, in_specs=in_specs, out_specs=out_specs, check_vma=False
    )
```
